32 devices in a mesh: section: 4 (over y, x), row: 4 (over z), col: 2 (over core).
Axes of the slice: x: 2, y: 2, z: 4, core: 2. Of those that a mesh axis runs over, the one named last changes fastest.
Arguments:
- stash: bfloat16 [4, 2, 1024, 6144], P('section', None, 'col', 'row'), may hold values from -6 to 6
- slot: int32 [4], P('section'), may hold values from 0 to 1
- cotangent: bfloat16 [4, 1024, 6144], P('section', 'col', 'row'), may hold values from -6 to 6
- w_first: bfloat16 [4, 6144, 14336], P('section', 'row', 'col'), may hold values from -0.109375 to 0.109375
- mask_first: int32 [4, 48, 112], P('section', 'row', 'col'), may hold values 0 or 1
- w_second: bfloat16 [4, 14336, 6144], P('section', 'col', 'row'), may hold values from -0.0625 to 0.0625
- mask_second: int32 [4, 112, 48], P('section', 'col', 'row'), may hold values 0 or 1
Outputs:
- grad_previous: bfloat16 [4, 1024, 6144], P('section', 'col', 'row')
- grad_first: bfloat16 [4, 6144, 14336], P('section', 'row', 'col')
- grad_second: bfloat16 [4, 14336, 6144], P('section', 'col', 'row')
The draws below stay inside these ranges and needn't reach their ends.
Inputs may be any that keep to these rules, and one draw needn't show every extreme that they name: `mask_first`: each entry is 0 (block absent) or 1 (block present). `mask_second`: each entry is 0 (block absent) or 1 (block present).
All inputs are finite; a program needn't handle non-finite values.
Results may differ from the reference program's by a relative error of at most 0.015.
Values may be sent and summed in bfloat16 or wider, within the bound.
A program may use at most 320 MiB of HBM per device.

```python
import jax
import jax.numpy as jnp
from jax import lax

D = 6144
FF = 14336
BLK = 128
MB = 1024
STASH = 2
DBLK = 48
FBLK = 112
N_SECTION = 4
N_ROW = 4
N_COL = 2


def plant(entries, rng, smallest, top_value):
    shape = entries.shape
    index_at = [jax.random.randint(jax.random.fold_in(rng, axis), (), 0, shape[axis]) for axis in range(len(shape))]
    entries = entries.at[tuple(index_at)].set(smallest)
    longest = shape.index(max(shape))
    index_at[longest] = (index_at[longest] + 1) % shape[longest]
    return entries.at[tuple(index_at)].set(top_value)


def levels(rng, dims, shards, low, top_value):
    factor_of = 1.0
    for dim, blocks in shards:
        steps = jax.random.uniform(jax.random.fold_in(jax.random.fold_in(rng, 6), dim), (blocks,), jnp.float32, low / len(shards), top_value / len(shards))
        factor_of = factor_of * jnp.repeat(jnp.exp(steps), dims[dim] // blocks).reshape((-1,) + (1,) * (len(dims) - 1 - dim))
    return factor_of


def noise(stream_key, shape, scale, most, split=(), kind=jnp.bfloat16):
    entries = scale * jax.random.normal(stream_key, shape, jnp.float32)
    if split:
        entries = entries * levels(stream_key, shape, split, -0.22, 0.18)
    return jnp.clip(entries, -most, most).astype(kind)


def setup_inputs(seed: int = 0) -> dict:
    keys = jax.random.split(jax.random.key(seed), 8)
    stash = noise(keys[0], (N_SECTION, STASH, MB, D), 1.0, 6.0, ((0, 4), (2, 2), (3, 4)))
    slot = plant(jax.random.randint(keys[1], (N_SECTION,), 0, STASH), jax.random.fold_in(keys[1], 1), 0, STASH - 1).astype(jnp.int32)
    cotangent = noise(keys[2], (N_SECTION, MB, D), 1.0, 6.0, ((0, 4), (1, 2), (2, 4)))
    w_first = noise(keys[3], (N_SECTION, D, FF), (D // 2) ** -0.5, 0.109375, ((0, 4), (1, 4), (2, 2)))
    mask_first = plant((jax.random.randint(keys[4], (N_SECTION, DBLK, FBLK), 0, 2) < 1).astype(jnp.int32), jax.random.fold_in(keys[4], 1), 0, 1)
    w_second = noise(keys[5], (N_SECTION, FF, D), (FF // 2) ** -0.5, 0.0625, ((0, 4), (1, 2), (2, 4)))
    mask_second = plant((jax.random.randint(keys[6], (N_SECTION, FBLK, DBLK), 0, 2) < 1).astype(jnp.int32), jax.random.fold_in(keys[6], 1), 0, 1)
    return {"stash": stash, "slot": slot, "cotangent": cotangent, "w_first": w_first, "mask_first": mask_first, "w_second": w_second, "mask_second": mask_second}


def apply_blocks(weight, blocks_on):
    height, breadth = weight.shape
    shaped = weight.reshape(height // BLK, BLK, breadth // BLK, BLK)
    shaped = shaped * blocks_on.astype(weight.dtype)[:, None, :, None]
    return shaped.reshape(height, breadth)


def banded(left, right, bands):
    width = left.shape[1] // bands
    total = jnp.zeros((left.shape[0], right.shape[1]), jnp.float32)
    for index in range(bands):
        part = jnp.dot(left[:, index * width:(index + 1) * width], right[index * width:(index + 1) * width, :], preferred_element_type=jnp.float32)
        total = total + part.astype(jnp.bfloat16).astype(jnp.float32)
    return total


def one_section(packed):
    saved, choose, upstream, first_raw, first_mask, second_raw, second_mask = packed
    inputs = lax.dynamic_index_in_dim(saved, choose.astype(jnp.int32), 0, keepdims=False)
    sparse_first = apply_blocks(first_raw, first_mask)
    sparse_second = apply_blocks(second_raw, second_mask)
    preact = banded(inputs, sparse_first, N_ROW)
    back = banded(upstream, sparse_second.T, N_ROW)
    sigmoid_val = jax.nn.sigmoid(preact)
    hidden = (preact * sigmoid_val).astype(jnp.bfloat16)
    hidden_grad = (back * sigmoid_val * (1.0 + preact * (1.0 - sigmoid_val))).astype(jnp.bfloat16)
    grad_first = apply_blocks(jnp.dot(inputs.T, hidden_grad, preferred_element_type=jnp.float32), first_mask).astype(jnp.bfloat16)
    grad_second = apply_blocks(jnp.dot(hidden.T, upstream, preferred_element_type=jnp.float32), second_mask).astype(jnp.bfloat16)
    input_grad = (upstream.astype(jnp.float32) + banded(hidden_grad, sparse_first.T, N_COL)).astype(jnp.bfloat16)
    return input_grad, grad_first, grad_second


def reference(stash, slot, cotangent, w_first, mask_first, w_second, mask_second):
    input_grad, grad_first, grad_second = lax.map(one_section, (stash, slot, cotangent, w_first, mask_first, w_second, mask_second))
    grad_previous = jnp.roll(input_grad, -1, axis=0)
    return grad_previous, grad_first, grad_second
```

```python
import jax
import jax.numpy as jnp
from jax import lax
from jax.sharding import PartitionSpec as P

BLK = 128
MOST_CHUNKS = 14


def masked(weight, blocks_on):
    height, breadth = weight.shape
    shaped = weight.reshape(height // BLK, BLK, breadth // BLK, BLK)
    on = (blocks_on != 0)[:, None, :, None]
    return jnp.where(on, shaped, jnp.zeros_like(shaped)).reshape(height, breadth)


def contract(left, right, left_dim, right_dim):
    return lax.dot_general(
        left, right, (((left_dim,), (right_dim,)), ((), ())), preferred_element_type=jnp.float32
    )


def pick(place, options):
    chosen = None
    for key, value in options:
        if chosen is None:
            chosen = jnp.where(place == key, value, jnp.zeros_like(value))
        else:
            chosen = jnp.where(place == key, value, chosen)
    return chosen


class Line:
    def __init__(self, count, size, upward):
        me = lax.axis_index("row")
        self.count, self.size, self.upward = count, size, upward
        self.place = me if upward else size - 1 - me
        self.came = []

    def device(self, place):
        return place if self.upward else self.size - 1 - place

    def slot(self, partials):
        t = len(self.came)
        senders = [k for k in range(self.size - 1) if 0 <= t - k < self.count]
        send = pick(self.place, [(k, partials[t - k]) for k in senders])
        if t:
            send = (send.astype(jnp.float32) + self.came[-1].astype(jnp.float32)).astype(
                send.dtype
            )
        route = [(self.device(k), self.device(k + 1)) for k in senders]
        self.came.append(lax.ppermute(send, "row", route))

    def before(self, chunk):
        return pick(self.place, [(k, self.came[chunk + k - 1]) for k in range(1, self.size)])


def on_device(stash, slot, cotangent, w_first, mask_first, w_second, mask_second):
    n_row, n_col = lax.axis_size("row"), lax.axis_size("col")
    upstream = cotangent[0]
    inputs = lax.dynamic_index_in_dim(stash[0], slot[0], 0, keepdims=False)
    first, second = w_first[0], w_second[0]
    on_first, on_second = mask_first[0], mask_second[0]
    swap = [(0, 1), (1, 0)]
    if n_col == 2:
        tokens_up = jnp.concatenate([upstream, lax.ppermute(upstream, "col", swap)], axis=0)
        tokens_in = jnp.concatenate([inputs, lax.ppermute(inputs, "col", swap)], axis=0)
    else:
        tokens_up = lax.all_gather(upstream, "col", axis=0, tiled=True)
        tokens_in = lax.all_gather(inputs, "col", axis=0, tiled=True)

    blocks = on_first.shape[1]
    count = max(n for n in range(1, min(blocks, MOST_CHUNKS) + 1) if blocks % n == 0)
    per = blocks // count
    width = per * BLK
    height = first.shape[0]

    sparse_first, pre_parts, back_parts = [], [], []
    lines = {(name, up): Line(count, n_row, up) for name in ("back", "pre") for up in (True, False)}
    grad_first = jnp.zeros(first.shape, jnp.bfloat16)
    grad_second = jnp.zeros(second.shape, jnp.bfloat16)
    total_input = None
    for t in range(count + n_row - 1):
        if t < count:
            cols, blks = slice(t * width, (t + 1) * width), slice(t * per, (t + 1) * per)
            second_c = masked(second[cols], on_second[blks])
            back_parts.append(contract(tokens_up, second_c, 1, 1).astype(jnp.bfloat16))
            first_c = masked(first[:, cols], on_first[:, blks])
            sparse_first.append(first_c)
            pre_parts.append(contract(tokens_in, first_c, 1, 0).astype(jnp.bfloat16))
        if t < count + n_row - 2:
            for name, parts in (("back", back_parts), ("pre", pre_parts)):
                for up in (True, False):
                    lines[name, up].slot(parts)
        c = t - (n_row - 1)
        if c < 0:
            continue

        def total(name, parts):
            whole = parts[c].astype(jnp.float32)
            if n_row > 1:
                for up in (True, False):
                    whole = whole + lines[name, up].before(c).astype(jnp.float32)
            return whole

        preact, back = total("pre", pre_parts), total("back", back_parts)
        gate = jax.nn.sigmoid(preact)
        hidden = (preact * gate).astype(jnp.bfloat16)
        hidden_grad = (back * gate * (1.0 + preact * (1.0 - gate))).astype(jnp.bfloat16)
        blks = slice(c * per, (c + 1) * per)
        term = contract(hidden_grad, sparse_first[c], 1, 1)
        total_input = term if total_input is None else total_input + term
        part = masked(contract(tokens_in, hidden_grad, 0, 0), on_first[:, blks])
        grad_first = lax.dynamic_update_slice(
            grad_first, part.astype(jnp.bfloat16), (0, c * width)
        )
        part = masked(contract(hidden, tokens_up, 0, 0), on_second[blks])
        grad_second = lax.dynamic_update_slice(
            grad_second, part.astype(jnp.bfloat16), (c * width, 0)
        )

    rounded = total_input.astype(jnp.bfloat16)
    if n_col == 2:
        half = upstream.shape[0]
        other = lax.ppermute(rounded[half:], "col", swap)
        summed = rounded[:half].astype(jnp.float32) + other.astype(jnp.float32)
    else:
        summed = lax.psum_scatter(rounded, "col", scatter_dimension=0, tiled=True).astype(
            jnp.float32
        )
    input_grad = (upstream.astype(jnp.float32) + summed).astype(jnp.bfloat16)
    n_section = lax.axis_size("section")
    moved = lax.ppermute(
        input_grad, "section", [((i + 1) % n_section, i) for i in range(n_section)]
    )
    return moved[None], grad_first[None], grad_second[None]


def solution(mesh):
    return jax.shard_map(
        on_device,
        mesh=mesh,
        in_specs=(
            P("section", None, "col", "row"),
            P("section"),
            P("section", "col", "row"),
            P("section", "row", "col"),
            P("section", "row", "col"),
            P("section", "col", "row"),
            P("section", "col", "row"),
        ),
        out_specs=(
            P("section", "col", "row"),
            P("section", "row", "col"),
            P("section", "col", "row"),
        ),
        check_vma=False,
    )
```
